32 devices in a mesh: row: 8 (over z, x), col: 4 (over y, core).
Axes of the slice: x: 2, y: 2, z: 4, core: 2. Of those that a mesh axis runs over, the one named last changes fastest.
Arguments:
- diag_inverse: bfloat16 [2, 8192, 8192], P(None, 'col', 'row'), as said below
- panel_rhs: bfloat16 [2, 8192, 128], P(None, 'row'), may hold values from -6 to 6
- below: bfloat16 [2, 22528, 8192], P(None, 'row', 'col'), may hold values from -0.03125 to 0.03125
- row_ids: int32 [2, 176], P(None, 'row'), may hold values from 0 to 256, as said below
- ancestor_rhs: bfloat16 [24576, 128], P(('row', 'col')), may hold values from -6 to 6
- ancestor_solution: bfloat16 [24576, 128], P(('row', 'col')), may hold values from -6 to 6
Outputs:
- solution: bfloat16 [2, 8192, 128], P(None, ('row', 'col'))
- rhs_updated: bfloat16 [24576, 128], P(('row', 'col'))
The draws below stay inside these ranges and needn't reach their ends.
Inputs may be any that keep to these rules, and one draw needn't show every extreme that they name: diag_inverse[p] is lower triangular with a positive diagonal. `row_ids`: slots 22 r to 22 r + 21 of either panel belong to the r-th index of row. Each holds 256 (empty) or a later block row that this index owns: for panel 0 a panel-1 block row in [r * 8, r * 8 + 8) or a value in [64 + r * 24, 64 + r * 24 + 24); for panel 1 only the latter. Live ids of one panel are distinct. In each panel some index of row has all 22 slots live.
All inputs are finite; a program needn't handle non-finite values.
Results may differ from the reference program's by a relative error of at most 0.017.
Values may be sent and summed in bfloat16 or wider, within the bound.
A program may use at most 128 MiB of HBM per device.

```python
import jax
import jax.numpy as jnp
from jax import lax

BS = 128
NRHS = 128
PW = 64
CAP = 22
NA_R = 24
COLS = 8192
NA = 192
SLOTS = 176
LATER = 256
N_ROW = 8


def draw_diag_inverse(key, part):
    noise_key, scale_key = jax.random.split(key)
    row_grid = lax.broadcasted_iota(jnp.int32, (2, COLS, COLS), 1)
    col_grid = lax.broadcasted_iota(jnp.int32, (2, COLS, COLS), 2)
    lower_part = jax.random.normal(noise_key, (2, COLS, COLS), jnp.float32)
    diagonal = jax.random.uniform(scale_key, (2, COLS, 1), jnp.float32, 0.7, 1.4)
    values = jnp.where(row_grid > col_grid, lower_part * COLS ** (-0.5), 0.0)
    values = values + jnp.where(row_grid == col_grid, diagonal, 0.0)
    return values.astype(jnp.bfloat16)


def draw_row_ids(key, part):
    panels = []
    pw_rows = PW // N_ROW
    for panel_index in range(2):
        panel_key = jax.random.fold_in(key, 7 + panel_index)
        full_key, count_key, owner_key = jax.random.split(panel_key, 3)
        full_owner = jax.random.randint(full_key, (), 0, N_ROW)
        low_owner = (full_owner + 1) % N_ROW
        owners = jnp.arange(N_ROW, dtype=jnp.int32)
        counts = jax.random.randint(count_key, (N_ROW,), CAP // 4, CAP + 1)
        counts = jnp.where(owners == full_owner, CAP, jnp.where(owners == low_owner, CAP // 4, counts))
        panel_extra = pw_rows if panel_index == 0 else 0
        candidates = panel_extra + NA_R

        def one_owner(owner_seed, owner_index, live_count):
            pick_key, place_key = jax.random.split(owner_seed)
            picked = jax.random.permutation(pick_key, candidates)[:CAP]
            position = jax.random.permutation(place_key, CAP)
            slot_ids = jnp.where(picked < panel_extra, owner_index * pw_rows + picked, PW + owner_index * NA_R + picked - panel_extra)
            return jnp.where(position < live_count, slot_ids, PW + NA_R * N_ROW)
        owner_keys = jax.random.split(owner_key, N_ROW)
        slots_all = jax.vmap(one_owner)(owner_keys, owners, counts)
        panels.append(slots_all.reshape(N_ROW * CAP))
    return jnp.stack(panels).astype(jnp.int32)


def level_of(rng, shape, cuts, least, largest):
    def one(dim, blocks):
        draws = jax.random.uniform(jax.random.fold_in(jax.random.fold_in(rng, 6), dim), (blocks,), jnp.float32, least / len(cuts), largest / len(cuts))
        return jnp.repeat(jnp.exp(draws), shape[dim] // blocks).reshape((-1,) + (1,) * (len(shape) - dim - 1))

    loudness = one(*cuts[0])
    for cut in cuts[1:]:
        loudness = loudness * one(*cut)
    return loudness


def scatter_about(rng, extent, deviation, most, cuts=(), held_as=jnp.bfloat16):
    level = level_of(rng, extent, cuts, -0.22, 0.18) if cuts else 1.0
    entries = jax.random.normal(rng, extent, jnp.float32) * deviation * level
    return jnp.minimum(jnp.maximum(entries, -most), most).astype(held_as)


def setup_inputs(seed: int = 0) -> dict:
    key_of = jax.random.split(jax.random.key(seed), 7)
    return {
        "diag_inverse": draw_diag_inverse(jax.random.fold_in(key_of[6], 71), 0),
        "panel_rhs": scatter_about(key_of[1], (2, COLS, NRHS), 1.0, 6.0, ((1, 8),)),
        "below": scatter_about(key_of[2], (2, SLOTS * BS, COLS), (4 * PW * BS) ** -0.5, 0.03125, ((1, 8), (2, 4))),
        "row_ids": draw_row_ids(jax.random.fold_in(key_of[6], 71), 0),
        "ancestor_rhs": scatter_about(key_of[4], (NA * BS, NRHS), 1.0, 6.0, ((0, 32),)),
        "ancestor_solution": scatter_about(key_of[5], (NA * BS, NRHS), 1.0, 6.0, ((0, 32),)),
    }


def slot_terms(factor_panel, solved, slot_ids):
    owner_blocks = factor_panel.reshape(N_ROW, CAP * BS, COLS)
    products = lax.map(lambda owner_rows: jnp.dot(owner_rows, solved, preferred_element_type=jnp.float32), owner_blocks)
    products = products.reshape(SLOTS, BS, NRHS)
    summed = jax.ops.segment_sum(products, slot_ids, num_segments=LATER + 1)
    return summed[:LATER]


def back_terms(factor_panel, known, slot_ids):
    gathered = known[slot_ids].reshape(N_ROW, CAP * BS, NRHS)
    owner_blocks = factor_panel.reshape(N_ROW, CAP * BS, COLS)

    def owner_product(pair_in):
        return lax.dot_general(pair_in[0], pair_in[1], (((0,), (0,)), ((), ())), preferred_element_type=jnp.float32)

    products = lax.map(owner_product, (owner_blocks, gathered))
    return jnp.sum(products, axis=0)


def reference(diag_inverse, panel_rhs, below, row_ids, ancestor_rhs, ancestor_solution):
    forward_zero = jnp.dot(diag_inverse[0], panel_rhs[0], preferred_element_type=jnp.float32).astype(jnp.bfloat16)
    later_zero = slot_terms(below[0], forward_zero, row_ids[0])
    panel_part = later_zero[:PW].reshape(COLS, NRHS)
    panel_one_rhs = (panel_rhs[1].astype(jnp.float32) - panel_part).astype(jnp.bfloat16)
    forward_one = jnp.dot(diag_inverse[1], panel_one_rhs, preferred_element_type=jnp.float32).astype(jnp.bfloat16)
    later_one = slot_terms(below[1], forward_one, row_ids[1])
    update = (later_zero[PW:] + later_one[PW:]).reshape(NA * BS, NRHS)
    rhs_updated = (ancestor_rhs.astype(jnp.float32) - update).astype(jnp.bfloat16)
    ancestor_blocks = ancestor_solution.reshape(NA, BS, NRHS)
    empty_panel = jnp.zeros((PW, BS, NRHS), jnp.bfloat16)
    empty_slot = jnp.zeros((1, BS, NRHS), jnp.bfloat16)
    known_one = jnp.concatenate([empty_panel, ancestor_blocks, empty_slot], axis=0)
    back_one_terms = back_terms(below[1], known_one, row_ids[1])
    back_one_rhs = (forward_one.astype(jnp.float32) - back_one_terms).astype(jnp.bfloat16)
    solution_one = jnp.dot(diag_inverse[1].T, back_one_rhs, preferred_element_type=jnp.float32).astype(jnp.bfloat16)
    known_zero = jnp.concatenate([solution_one.reshape(PW, BS, NRHS), ancestor_blocks, empty_slot], axis=0)
    back_zero_terms = back_terms(below[0], known_zero, row_ids[0])
    back_zero_rhs = (forward_zero.astype(jnp.float32) - back_zero_terms).astype(jnp.bfloat16)
    solution_zero = jnp.dot(diag_inverse[0].T, back_zero_rhs, preferred_element_type=jnp.float32).astype(jnp.bfloat16)
    solution = jnp.stack([solution_zero, solution_one])
    return solution, rhs_updated
```

```python
import functools

import jax
import jax.numpy as jnp
from jax import lax
from jax.experimental import pallas as pl
from jax.experimental.pallas import tpu as pltpu
from jax.sharding import PartitionSpec as P

MESH = pl.DeviceIdType.MESH
BF = jnp.bfloat16
F32 = jnp.float32


def sizes_of(n, m, diag, panel_rhs, below, row_ids, ancestor_rhs):
    z = {}
    z["n"], z["m"] = n, m
    z["nz"] = n // 2
    z["cc"], z["p"] = diag.shape[1], diag.shape[2]
    z["nrhs"] = panel_rhs.shape[2]
    z["cap"] = row_ids.shape[1]
    z["bs"] = below.shape[1] // z["cap"]
    z["b"] = z["cc"] // n
    z["q"] = z["p"] // m
    z["a"] = ancestor_rhs.shape[0]
    z["ab"] = z["a"] // z["bs"]
    z["na"] = z["ab"] * m
    z["pb"] = z["p"] // z["bs"]
    z["pw"] = z["cc"] * m // z["bs"]
    return z


def kernel(
    z, idx, d_hbm, prhs, b_hbm, arhs, asol, sol, upd,
    vd0, vd1, vb0, vb1, bp, known, vt, slots, accT,
    part_f0, part_b1, part_f1, part_b0, full_f0, full_b1, full_f1, full_b0,
    xr, zs, zr, part_p, full_p, part_s1, full_s1, part_s0, part_u, cr, cru,
    lsem, ssem, rsem,
):
    n, m, nz, b, q = z["n"], z["m"], z["nz"], z["b"], z["q"]
    cc, cap, bs, nrhs, na, pb = z["cc"], z["cap"], z["bs"], z["nrhs"], z["na"], z["pb"]
    ab, a = z["ab"], z["a"]
    me = lax.axis_index("row")
    mc = lax.axis_index("col")
    par = lax.rem(me, 2)
    zi = me // 2
    partner = me + 1 - 2 * par
    o_pan, o_l0, o_l1, o_p0, o_p1 = 0, pb, pb + na, pb + 2 * na, pb + 2 * na + cap

    counter = [0]
    pending = []

    def send(src, dst, axis, place, slot):
        cp = pltpu.make_async_remote_copy(
            src_ref=src, dst_ref=dst, send_sem=ssem.at[slot], recv_sem=rsem.at[slot],
            device_id={axis: place}, device_id_type=MESH,
        )
        cp.start()
        pending.append(cp)
        return cp

    def take(count):
        base = counter[0]
        counter[0] += count
        return base

    def rows(ref, block, size):
        return ref.at[pl.ds(pl.multiple_of(block * size, size), size)]

    def get(ref, block, size):
        return ref[pl.ds(pl.multiple_of(block * size, size), size), :]

    def put(ref, block, size, value):
        ref[pl.ds(pl.multiple_of(block * size, size), size), :] = value

    class RowSum:
        def __init__(self, which, part):
            self.w, self.part = which, part
            self.xs, self.zs = take(nz), take(nz)
            self.xc, self.zc = {}, {}

        def send_x(self, j):
            zd = lax.rem(zi + j, nz)
            self.xc[j] = send(
                rows(self.part, zd * 2 + 1 - par, b), xr.at[self.w, j], "row", partner, self.xs + j
            )

        def forward(self):
            for j in range(1, nz):
                zd = lax.rem(zi + j, nz)
                self.xc[j].wait_recv()
                both = get(self.part, zd * 2 + par, b).astype(F32) + xr[self.w, j].astype(F32)
                zs[self.w, j] = both.astype(BF)
                self.zc[j] = send(
                    zs.at[self.w, j], zr.at[self.w, j], "row", zd * 2 + par, self.zs + j
                )

        def finish(self):
            self.xc[0].wait_recv()
            total = get(self.part, me, b).astype(F32) + xr[self.w, 0].astype(F32)
            for j in range(1, nz):
                self.zc[j].wait_recv()
                total = total + zr[self.w, j].astype(F32)
            return total

    class RowGather:
        def __init__(self, full):
            self.full = full
            self.xs, self.zs = take(nz), take(nz)
            self.xc, self.zc = {}, {}

        def start(self):
            mine = rows(self.full, me, b)
            self.xc[0] = send(mine, mine, "row", partner, self.xs)
            for j in range(1, nz):
                self.zc[j] = send(mine, mine, "row", lax.rem(zi + j, nz) * 2 + par, self.zs + j)

        def forward(self):
            for j in range(1, nz):
                self.zc[j].wait_recv()
                theirs = rows(self.full, lax.rem(zi + nz - j, nz) * 2 + par, b)
                self.xc[j] = send(theirs, theirs, "row", partner, self.xs + j)

        def finish(self):
            for j in range(nz):
                self.xc[j].wait_recv()

    class ColSum:
        def __init__(self, part, landing, size):
            self.part, self.landing, self.size = part, landing, size
            self.s = take(m)
            self.c = {}

        def start(self):
            for d in range(1, m):
                place = lax.rem(mc + d, m)
                self.c[d] = send(
                    rows(self.part, place, self.size), self.landing.at[d], "col", place, self.s + d
                )

        def finish(self):
            total = get(self.part, mc, self.size).astype(F32)
            for d in range(1, m):
                self.c[d].wait_recv()
                total = total + self.landing[d].astype(F32)
            return total

    class ColGather:
        def __init__(self, src, dst):
            self.src, self.dst = src, dst
            self.s = take(m)
            self.c = {}

        def start(self):
            for d in range(1, m):
                self.c[d] = send(self.src, self.dst, "col", lax.rem(mc + d, m), self.s + d)

        def finish(self):
            for d in range(1, m):
                self.c[d].wait_recv()

    load_d0 = pltpu.make_async_copy(d_hbm.at[0], vd0, lsem.at[0])
    load_b1 = pltpu.make_async_copy(b_hbm.at[1], vb1, lsem.at[1])
    load_b0 = pltpu.make_async_copy(b_hbm.at[0], vb0.at[pl.ds(0, cap)], lsem.at[2])
    load_d1 = pltpu.make_async_copy(d_hbm.at[1], vd1, lsem.at[3])
    for load in (load_d0, load_b1, load_b0, load_d1):
        load.start()

    barrier = pltpu.get_barrier_semaphore()
    peers = [{"row": partner}]
    peers += [{"row": lax.rem(zi + j, nz) * 2 + par} for j in range(1, nz)]
    peers += [{"col": lax.rem(mc + d, m)} for d in range(1, m)]
    for peer in peers:
        pl.semaphore_signal(barrier, inc=1, device_id=peer, device_id_type=MESH)
    pl.semaphore_wait(barrier, len(peers))

    gather_a = ColGather(asol, known.at[pl.ds(mc * ab, ab)])
    gather_a.start()

    def solve_forward(summing, vd, x):
        order = list(range(1, nz)) + [0]
        for j in order:
            block = lax.rem(zi + j, nz) * 2 + 1 - par
            value = jnp.dot(get(vd, block, b), x, preferred_element_type=F32)
            put(summing.part, block, b, value.astype(BF))
            summing.send_x(j)
        for j in order:
            block = lax.rem(zi + j, nz) * 2 + par
            value = jnp.dot(get(vd, block, b), x, preferred_element_type=F32)
            put(summing.part, block, b, value.astype(BF))

    sum_f0 = RowSum(0, part_f0)
    load_d0.wait()
    solve_forward(sum_f0, vd0, prhs[0])
    known[pl.ds(mc * ab, ab)] = asol[...]
    known[na] = jnp.zeros((bs, nrhs), BF)
    vb0[cap] = jnp.zeros((bs, cc), BF)
    slots[0, cap] = jnp.zeros((bs, nrhs), F32)
    slots[1, cap] = jnp.zeros((bs, nrhs), F32)
    sum_f0.forward()
    load_b0.wait()
    for k in range(pb):
        bp[k] = vb0[idx[o_pan + k]]
    f0_mine = sum_f0.finish().astype(BF)
    put(full_f0, me, b, f0_mine)
    gather_f0 = RowGather(full_f0)
    gather_f0.start()

    def gather_values(offset):
        for s in range(cap):
            block = known[idx[offset + s]].astype(F32)
            vt[:, s * bs:(s + 1) * bs] = block.T.astype(BF)

    tile = min(256, cc)
    tiles = cc // tile

    load_b1.wait()
    gather_a.finish()
    gather_values(o_p1)

    def back_tile(vb, t):
        cols = pl.ds(pl.multiple_of(t * tile, tile), tile)
        return jnp.dot(
            vt[...], vb[0:cap, :, cols].reshape(cap * bs, tile), preferred_element_type=F32
        )

    def one_tile(t, carry):
        put(part_b1, t, tile, back_tile(vb1, t).T.astype(BF))
        return carry

    lax.fori_loop(0, tiles // 2, one_tile, 0)
    gather_f0.forward()
    lax.fori_loop(tiles // 2, tiles, one_tile, 0)
    gather_f0.finish()

    sum_p = ColSum(part_p, cr.at[0], q)
    panel_tile = 2 if pb % 2 == 0 else 1

    def panel_step(t, carry):
        block = bp[pl.ds(t * panel_tile, panel_tile)].reshape(panel_tile * bs, cc)
        value = jnp.dot(block, full_f0[...], preferred_element_type=F32)
        put(part_p, t, panel_tile * bs, value.astype(BF))
        return carry

    lax.fori_loop(0, pb // panel_tile, panel_step, 0)
    sum_p.start()
    sum_b1 = RowSum(1, part_b1)
    for j in list(range(1, nz)) + [0]:
        sum_b1.send_x(j)
    p_part = sum_p.finish()
    p_rhs = prhs[1, pl.ds(pl.multiple_of(mc * q, q), q), :].astype(F32)
    put(full_p, mc, q, (p_rhs - p_part).astype(BF))
    gather_p = ColGather(rows(full_p, mc, q), rows(full_p, mc, q))
    gather_p.start()
    sum_b1.forward()
    load_d1.wait()
    gather_p.finish()

    sum_f1 = RowSum(2, part_f1)
    solve_forward(sum_f1, vd1, full_p[...])
    sum_f1.forward()
    gather_values(o_p0)

    def zero_tile(t, carry):
        accT[:, pl.ds(pl.multiple_of(t * tile, tile), tile)] = back_tile(vb0, t)
        return carry

    lax.fori_loop(0, tiles, zero_tile, 0)
    b1_mine = sum_b1.finish()
    f1_mine = sum_f1.finish().astype(BF)
    put(full_b1, me, b, (f1_mine.astype(F32) - b1_mine).astype(BF))
    gather_b1 = RowGather(full_b1)
    gather_b1.start()
    put(full_f1, me, b, f1_mine)
    gather_b1.forward()
    gather_f1 = RowGather(full_f1)
    gather_f1.start()
    gather_b1.finish()

    def solve_back(full, vd, part):
        xt = full[...].astype(F32).T.astype(BF)
        yt = jnp.dot(xt, vd[...], preferred_element_type=F32)
        part[...] = yt.T.astype(BF)

    sum_s1 = ColSum(part_s1, cr.at[1], q)
    solve_back(full_b1, vd1, part_s1)
    sum_s1.start()
    gather_f1.forward()
    s1_mine = sum_s1.finish().astype(BF)
    put(full_s1, mc, q, s1_mine)
    gather_s1 = ColGather(rows(full_s1, mc, q), rows(full_s1, mc, q))
    gather_s1.start()
    sol[1] = s1_mine
    gather_s1.finish()

    s1t = full_s1[...].astype(F32).T.astype(BF)
    vt[:, 0:pb * bs] = s1t

    def panel_back(t, carry):
        cols = pl.ds(pl.multiple_of(t * tile, tile), tile)
        value = jnp.dot(
            vt[:, 0:pb * bs], bp[:, :, cols].reshape(pb * bs, tile), preferred_element_type=F32
        )
        put(part_b0, t, tile, (value + accT[:, cols]).T.astype(BF))
        return carry

    lax.fori_loop(0, tiles, panel_back, 0)
    sum_b0 = RowSum(3, part_b0)
    for j in list(range(1, nz)) + [0]:
        sum_b0.send_x(j)
    group = 2 if cap % 2 == 0 else 1

    def later(which, vb, full):
        def step(t, carry):
            block = vb[pl.ds(t * group, group)].reshape(group * bs, cc)
            value = jnp.dot(block, full[...], preferred_element_type=F32)
            slots[which, pl.ds(t * group, group)] = value.reshape(group, bs, nrhs)
            return carry

        lax.fori_loop(0, cap // group, step, 0)

    sum_b0.forward()
    later(0, vb0, full_f0)
    b0_mine = sum_b0.finish()
    put(full_b0, me, b, (f0_mine.astype(F32) - b0_mine).astype(BF))
    gather_b0 = RowGather(full_b0)
    gather_b0.start()
    gather_b0.forward()
    gather_f1.finish()
    later(1, vb1, full_f1)
    for k in range(na):
        value = slots[0, idx[o_l0 + k]] + slots[1, idx[o_l1 + k]]
        part_u[k * bs:(k + 1) * bs, :] = value.astype(BF)
    gather_b0.finish()

    sum_s0 = ColSum(part_s0, cr.at[2], q)
    sum_u = ColSum(part_u, cru, a)
    solve_back(full_b0, vd0, part_s0)
    sum_s0.start()
    sum_u.start()
    sol[0] = sum_s0.finish().astype(BF)
    upd[...] = (arhs[...].astype(F32) - sum_u.finish()).astype(BF)
    for cp in pending:
        cp.wait_send()


def on_device(diag, panel_rhs, below, row_ids, ancestor_rhs, ancestor_solution):
    n, m = lax.axis_size("row"), lax.axis_size("col")
    z = sizes_of(n, m, diag, panel_rhs, below, row_ids, ancestor_rhs)
    nz, b, q = z["nz"], z["b"], z["q"]
    cc, p, cap, bs, nrhs, na, pb = (z[k] for k in ("cc", "p", "cap", "bs", "nrhs", "na", "pb"))
    a, ab = z["a"], z["ab"]
    row = lax.axis_index("row")

    def slot_of(ids, wanted):
        found = ids[None, :] == wanted[:, None]
        return jnp.min(jnp.where(found, jnp.arange(cap)[None, :], cap), axis=1)

    def place_of(ids):
        position = ids - z["pw"] - row * na
        return jnp.where((position >= 0) & (position < na), position, na)

    later_ids = z["pw"] + row * na + jnp.arange(na)
    idx = jnp.concatenate([
        slot_of(row_ids[0], row * pb + jnp.arange(pb)),
        slot_of(row_ids[0], later_ids),
        slot_of(row_ids[1], later_ids),
        place_of(row_ids[0]),
        place_of(row_ids[1]),
    ]).astype(jnp.int32)

    vmem = pl.BlockSpec(memory_space=pltpu.VMEM)
    hbm = pl.BlockSpec(memory_space=pl.ANY)
    nsem = 4 * 2 * nz + 4 * 2 * nz + 7 * m
    V = pltpu.VMEM
    return pl.pallas_call(
        functools.partial(kernel, z),
        out_shape=(
            jax.ShapeDtypeStruct((2, q, nrhs), BF),
            jax.ShapeDtypeStruct((a, nrhs), BF),
        ),
        in_specs=[pl.BlockSpec(memory_space=pltpu.SMEM), hbm, vmem, hbm, vmem, vmem],
        out_specs=(vmem, vmem),
        scratch_shapes=[
            V((cc, p), BF), V((cc, p), BF),
            V((cap + 1, bs, cc), BF), V((cap, bs, cc), BF), V((pb, bs, cc), BF),
            V((na + 1, bs, nrhs), BF), V((nrhs, max(cap, pb) * bs), BF),
            V((2, cap + 1, bs, nrhs), F32), V((nrhs, cc), F32),
        ] + [V((cc, nrhs), BF)] * 8 + [V((4, nz, b, nrhs), BF)] * 3 + [
            V((p, nrhs), BF), V((p, nrhs), BF), V((p, nrhs), BF), V((p, nrhs), BF),
            V((p, nrhs), BF), V((na * bs, nrhs), BF),
            V((3, m, q, nrhs), BF), V((m, a, nrhs), BF),
            pltpu.SemaphoreType.DMA((4,)),
            pltpu.SemaphoreType.DMA((nsem,)),
            pltpu.SemaphoreType.DMA((nsem,)),
        ],
        compiler_params=pltpu.CompilerParams(
            collective_id=0, has_side_effects=True, vmem_limit_bytes=62 * 1024 * 1024
        ),
    )(
        idx, diag, panel_rhs, below.reshape(2, cap, bs, cc), ancestor_rhs,
        ancestor_solution.reshape(ab, bs, nrhs),
    )


def solution(mesh):
    in_specs = (
        P(None, "col", "row"),
        P(None, "row", None),
        P(None, "row", "col"),
        P(None, "row"),
        P(("row", "col"), None),
        P(("row", "col"), None),
    )
    out_specs = (P(None, ("row", "col"), None), P(("row", "col"), None))
    return jax.shard_map(
        on_device, mesh=mesh, in_specs=in_specs, out_specs=out_specs, check_vma=False
    )
```

```python
import functools

import jax
import jax.numpy as jnp
from jax import lax
from jax.experimental import pallas as pl
from jax.experimental.pallas import tpu as pltpu
from jax.sharding import PartitionSpec as P

MESH = pl.DeviceIdType.MESH
BF = jnp.bfloat16
F32 = jnp.float32


def sizes_of(n, m, diag, panel_rhs, below, row_ids, ancestor_rhs):
    z = {}
    z["n"], z["m"] = n, m
    z["nz"] = n // 2
    z["cc"], z["p"] = diag.shape[1], diag.shape[2]
    z["nrhs"] = panel_rhs.shape[2]
    z["cap"] = row_ids.shape[1]
    z["bs"] = below.shape[1] // z["cap"]
    z["b"] = z["cc"] // n
    z["q"] = z["p"] // m
    z["a"] = ancestor_rhs.shape[0]
    z["ab"] = z["a"] // z["bs"]
    z["na"] = z["ab"] * m
    z["pb"] = z["p"] // z["bs"]
    z["pw"] = z["cc"] * m // z["bs"]
    return z


def kernel(
    z, idx, d_hbm, prhs, b_hbm, arhs, asol, sol, upd,
    vd0, vd1, vb0, vb1, bp, known, vt, slots, accT,
    part_b1, full_f1, wide, part_f0, part_f1, part_b0, full_f0, full_b1, full_b0,
    xr, zs, zr, xr1, zs1, zr1, part_p, full_p, part_s1, full_s1, part_s0, part_u, cr, cru,
    lsem, ssem, rsem,
):
    n, m, nz, b, q = z["n"], z["m"], z["nz"], z["b"], z["q"]
    cc, cap, bs, nrhs, na, pb = z["cc"], z["cap"], z["bs"], z["nrhs"], z["na"], z["pb"]
    ab, a = z["ab"], z["a"]
    me = lax.axis_index("row")
    mc = lax.axis_index("col")
    par = lax.rem(me, 2)
    zi = me // 2
    partner = me + 1 - 2 * par
    o_pan, o_l0, o_l1, o_p0, o_p1 = 0, pb, pb + na, pb + 2 * na, pb + 2 * na + cap

    counter = [0]
    pending = []

    def send(src, dst, axis, place, slot):
        cp = pltpu.make_async_remote_copy(
            src_ref=src, dst_ref=dst, send_sem=ssem.at[slot], recv_sem=rsem.at[slot],
            device_id={axis: place}, device_id_type=MESH,
        )
        cp.start()
        pending.append(cp)
        return cp

    def take(count):
        base = counter[0]
        counter[0] += count
        return base

    def rows(ref, block, size):
        return ref.at[pl.ds(pl.multiple_of(block * size, size), size)]

    def get(ref, block, size):
        return ref[pl.ds(pl.multiple_of(block * size, size), size), :]

    def put(ref, block, size, value):
        ref[pl.ds(pl.multiple_of(block * size, size), size), :] = value

    class RowSum:
        def __init__(self, part, size, xr, zs, zr):
            self.part, self.size = part, size
            self.xr, self.zs, self.zr = xr, zs, zr
            self.xk, self.zk = take(nz), take(nz)
            self.xc, self.zc = {}, {}

        def send_x(self, j):
            zd = lax.rem(zi + j, nz)
            self.xc[j] = send(
                rows(self.part, zd * 2 + 1 - par, self.size), self.xr.at[j], "row", partner,
                self.xk + j,
            )

        def forward(self):
            for j in range(1, nz):
                zd = lax.rem(zi + j, nz)
                self.xc[j].wait_recv()
                mine = get(self.part, zd * 2 + par, self.size)
                self.zs[j] = (mine.astype(F32) + self.xr[j].astype(F32)).astype(BF)
                self.zc[j] = send(
                    self.zs.at[j], self.zr.at[j], "row", zd * 2 + par, self.zk + j
                )

        def finish(self):
            self.xc[0].wait_recv()
            total = get(self.part, me, self.size).astype(F32) + self.xr[0].astype(F32)
            for j in range(1, nz):
                self.zc[j].wait_recv()
                total = total + self.zr[j].astype(F32)
            return total

    class RowGather:
        def __init__(self, full, size):
            self.full, self.size = full, size
            self.xk, self.zk = take(nz), take(nz)
            self.xc, self.zc = {}, {}

        def start(self):
            mine = rows(self.full, me, self.size)
            self.xc[0] = send(mine, mine, "row", partner, self.xk)
            for j in range(1, nz):
                self.zc[j] = send(mine, mine, "row", lax.rem(zi + j, nz) * 2 + par, self.zk + j)

        def forward(self):
            for j in range(1, nz):
                self.zc[j].wait_recv()
                theirs = rows(self.full, lax.rem(zi + nz - j, nz) * 2 + par, self.size)
                self.xc[j] = send(theirs, theirs, "row", partner, self.xk + j)

        def finish(self):
            for j in range(nz):
                self.xc[j].wait_recv()

    class ColSum:
        def __init__(self, part, landing, size):
            self.part, self.landing, self.size = part, landing, size
            self.s = take(m)
            self.c = {}

        def start(self):
            for d in range(1, m):
                place = lax.rem(mc + d, m)
                self.c[d] = send(
                    rows(self.part, place, self.size), self.landing.at[d], "col", place, self.s + d
                )

        def finish(self):
            total = get(self.part, mc, self.size).astype(F32)
            for d in range(1, m):
                self.c[d].wait_recv()
                total = total + self.landing[d].astype(F32)
            return total

    class ColGather:
        def __init__(self, src, dst):
            self.src, self.dst = src, dst
            self.s = take(m)
            self.c = {}

        def start(self):
            for d in range(1, m):
                self.c[d] = send(self.src, self.dst, "col", lax.rem(mc + d, m), self.s + d)

        def finish(self):
            for d in range(1, m):
                self.c[d].wait_recv()

    load_d0 = pltpu.make_async_copy(d_hbm.at[0], vd0, lsem.at[0])
    load_b1 = pltpu.make_async_copy(b_hbm.at[1], vb1, lsem.at[1])
    load_b0 = pltpu.make_async_copy(b_hbm.at[0], vb0.at[pl.ds(0, cap)], lsem.at[2])
    load_d1 = pltpu.make_async_copy(d_hbm.at[1], vd1, lsem.at[3])
    for load in (load_d0, load_b1, load_b0, load_d1):
        load.start()

    barrier = pltpu.get_barrier_semaphore()
    peers = [{"row": partner}]
    peers += [{"row": lax.rem(zi + j, nz) * 2 + par} for j in range(1, nz)]
    peers += [{"col": lax.rem(mc + d, m)} for d in range(1, m)]
    for peer in peers:
        pl.semaphore_signal(barrier, inc=1, device_id=peer, device_id_type=MESH)
    pl.semaphore_wait(barrier, len(peers))

    gather_a = ColGather(asol, known.at[pl.ds(mc * ab, ab)])
    gather_a.start()

    hb, hq, hn = b // 2, q // 2, nrhs // 2

    def pack(value, size):
        blocks = value.reshape(-1, size, hn)
        half = size // 2
        both = jnp.concatenate([blocks[:, :half], blocks[:, half:]], axis=2)
        return both.reshape(-1, nrhs)

    def unpack(value, size):
        half = size // 2
        blocks = value.astype(F32).reshape(-1, half, nrhs)
        both = jnp.concatenate([blocks[:, :, :hn], blocks[:, :, hn:]], axis=1)
        return both.reshape(-1, hn)

    def part_of(value, h):
        return value[:, h * hn:(h + 1) * hn]

    order = list(range(1, nz)) + [0]
    tile = max(min(256, cc), b)
    tiles = cc // tile

    sum_f0 = [RowSum(part_f0.at[h], hb, xr.at[0, h], zs.at[0, h], zr.at[0, h]) for h in range(2)]
    sum_f1 = [RowSum(part_f1.at[h], hb, xr.at[1, h], zs.at[1, h], zr.at[1, h]) for h in range(2)]
    sum_b0 = [RowSum(part_b0.at[h], hb, xr.at[2, h], zs.at[2, h], zr.at[2, h]) for h in range(2)]
    sum_b1 = RowSum(part_b1, b, xr1, zs1, zr1)
    gather_f0 = [RowGather(full_f0.at[h], hb) for h in range(2)]
    gather_b1 = [RowGather(full_b1.at[h], hb) for h in range(2)]
    gather_b0 = [RowGather(full_b0.at[h], hb) for h in range(2)]
    gather_f1 = RowGather(full_f1, b)
    sum_p = [ColSum(part_p.at[h], cr.at[0, h], hq) for h in range(2)]
    sum_s1 = [ColSum(part_s1.at[h], cr.at[1, h], hq) for h in range(2)]
    sum_s0 = [ColSum(part_s0.at[h], cr.at[2, h], hq) for h in range(2)]
    sum_u = ColSum(part_u, cru, a)

    def col_gather(full, h):
        mine = rows(full.at[h], mc, hq)
        return ColGather(mine, mine)

    gather_p = [col_gather(full_p, h) for h in range(2)]
    gather_s1 = [col_gather(full_s1, h) for h in range(2)]

    load_d0.wait()
    x0 = prhs[0]
    for j in order:
        block = lax.rem(zi + j, nz) * 2 + 1 - par
        value = jnp.dot(get(vd0, block, b), x0, preferred_element_type=F32)
        for h in range(2):
            put(part_f0.at[h], block, hb, pack(part_of(value, h), b).astype(BF))
        sum_f0[0].send_x(j)
    for j in order:
        sum_f0[1].send_x(j)
    for j in order:
        block = lax.rem(zi + j, nz) * 2 + par
        value = jnp.dot(get(vd0, block, b), x0, preferred_element_type=F32)
        for h in range(2):
            put(part_f0.at[h], block, hb, pack(part_of(value, h), b).astype(BF))
    known[pl.ds(mc * ab, ab)] = asol[...]
    known[na] = jnp.zeros((bs, nrhs), BF)
    vb0[cap] = jnp.zeros((bs, cc), BF)
    slots[0, cap] = jnp.zeros((bs, nrhs), F32)
    slots[1, cap] = jnp.zeros((bs, nrhs), F32)

    def gather_values(offset):
        for s in range(cap):
            block = known[idx[offset + s]].astype(F32)
            vt[:, s * bs:(s + 1) * bs] = block.T.astype(BF)

    def back_tile(vb, t):
        cols = pl.ds(pl.multiple_of(t * tile, tile), tile)
        return jnp.dot(
            vt[:, 0:cap * bs], vb[0:cap, :, cols].reshape(cap * bs, tile),
            preferred_element_type=F32,
        )

    def one_tile(t, carry):
        put(part_b1, t, tile, back_tile(vb1, t).T.astype(BF))
        return carry

    def zero_tile(t, carry):
        accT[:, pl.ds(pl.multiple_of(t * tile, tile), tile)] = back_tile(vb0, t)
        return carry

    group = 2 if cap % 2 == 0 else 1

    def later(which, vb):
        def step(t, carry):
            block = vb[pl.ds(t * group, group)].reshape(group * bs, cc)
            value = jnp.dot(block, wide[which], preferred_element_type=F32)
            slots[which, pl.ds(t * group, group)] = value.reshape(group, bs, nrhs)
            return carry

        lax.fori_loop(0, cap // group, step, 0)

    def solve_forward(summing, h, vd, x):
        for j in order:
            block = lax.rem(zi + j, nz) * 2 + 1 - par
            value = jnp.dot(get(vd, block, b), x, preferred_element_type=F32)
            put(summing.part, block, hb, pack(value, b).astype(BF))
            summing.send_x(j)
        for j in order:
            block = lax.rem(zi + j, nz) * 2 + par
            value = jnp.dot(get(vd, block, b), x, preferred_element_type=F32)
            put(summing.part, block, hb, pack(value, b).astype(BF))

    def solve_back(full, h, vd, part):
        xt = unpack(full[h], b).T.astype(BF)
        yt = jnp.dot(xt, vd[...], preferred_element_type=F32)
        part[h] = pack(yt.T, q).astype(BF)

    panel_tile = 2 if pb % 2 == 0 else 1
    held = {}

    def chain(h):
        sum_f0[h].forward()
        yield
        f0_mine = sum_f0[h].finish().astype(BF)
        put(full_f0.at[h], me, hb, f0_mine)
        gather_f0[h].start()
        yield
        gather_f0[h].forward()
        yield
        gather_f0[h].finish()
        x = unpack(full_f0[h], b).astype(BF)
        held["f0", h] = x

        for t in range(pb // panel_tile):
            block = bp[t * panel_tile:(t + 1) * panel_tile].reshape(panel_tile * bs, cc)
            value = jnp.dot(block, x, preferred_element_type=F32)
            put(part_p.at[h], t, panel_tile * bs // 2, pack(value, q).astype(BF))
        sum_p[h].start()
        yield
        p_part = sum_p[h].finish()
        mine = prhs[1, pl.ds(pl.multiple_of(mc * q, q), q), :].astype(F32)
        put(full_p.at[h], mc, hq, (pack(part_of(mine, h), q) - p_part).astype(BF))
        gather_p[h].start()
        yield
        gather_p[h].finish()
        solve_forward(sum_f1[h], h, vd1, unpack(full_p[h], q).astype(BF))
        yield
        sum_f1[h].forward()
        yield
        f1_mine = sum_f1[h].finish().astype(BF)
        put(full_b1.at[h], me, hb, (f1_mine.astype(F32) - held["b1"][h]).astype(BF))
        gather_b1[h].start()
        put(full_f1, me * 2 + h, hb, f1_mine)
        yield
        gather_b1[h].forward()
        yield
        gather_b1[h].finish()
        solve_back(full_b1, h, vd1, part_s1)
        sum_s1[h].start()
        yield
        put(full_s1.at[h], mc, hq, sum_s1[h].finish().astype(BF))
        gather_s1[h].start()
        yield
        gather_s1[h].finish()
        s1t = unpack(full_s1[h], q).T.astype(BF)
        for t in range(tiles):
            cols = slice(t * tile, (t + 1) * tile)
            value = jnp.dot(
                s1t, bp[:, :, cols].reshape(pb * bs, tile), preferred_element_type=F32
            )
            value = (value + accT[h * hn:(h + 1) * hn, cols]).T
            put(part_b0.at[h], t, tile // 2, pack(value, b).astype(BF))
        for j in order:
            sum_b0[h].send_x(j)
        yield
        sum_b0[h].forward()
        yield
        b0_mine = sum_b0[h].finish()
        put(full_b0.at[h], me, hb, (f0_mine.astype(F32) - b0_mine).astype(BF))
        gather_b0[h].start()
        yield
        gather_b0[h].forward()
        yield
        gather_b0[h].finish()
        solve_back(full_b0, h, vd0, part_s0)
        sum_s0[h].start()
        yield

    half_tiles = tiles // 2

    def beside_f0_sum():
        load_b0.wait()
        for k in range(pb):
            bp[k] = vb0[idx[o_pan + k]]

    def beside_f0_gather():
        load_b1.wait()
        gather_a.finish()
        gather_values(o_p1)
        lax.fori_loop(0, half_tiles, one_tile, 0)

    def rest_of_b1():
        lax.fori_loop(half_tiles, tiles, one_tile, 0)

    def send_b1():
        for j in order:
            sum_b1.send_x(j)
        wide[0] = jnp.concatenate([held["f0", 0], held["f0", 1]], axis=1)

    def forward_b1():
        sum_b1.forward()
        gather_values(o_p0)
        load_d1.wait()

    def first_ancestors():
        lax.fori_loop(0, half_tiles, zero_tile, 0)

    def rest_of_ancestors():
        lax.fori_loop(half_tiles, tiles, zero_tile, 0)
        total = sum_b1.finish()
        held["b1"] = [pack(part_of(total, h), b) for h in range(2)]

    def later_zero():
        later(0, vb0)

    def later_one():
        gather_f1.finish()
        blocks = full_f1[...].reshape(n, 2, hb, nrhs)
        wide[1] = jnp.concatenate(
            [unpack(blocks[:, h].reshape(n * hb, nrhs), b).astype(BF) for h in range(2)], axis=1
        )
        later(1, vb1)
        for k in range(na):
            value = slots[0, idx[o_l0 + k]] + slots[1, idx[o_l1 + k]]
            part_u[k * bs:(k + 1) * bs, :] = value.astype(BF)
        sum_u.start()

    beside = [
        beside_f0_sum, beside_f0_gather, rest_of_b1, send_b1, forward_b1, first_ancestors,
        rest_of_ancestors, later_zero, gather_f1.start, gather_f1.forward, None, None,
        later_one, None, None, None,
    ]
    chains = [chain(0), chain(1)]
    for extra in beside:
        for one in chains:
            next(one)
        if extra is not None:
            extra()

    for which, done in ((1, full_s1), (0, None)):
        halves = []
        for h in range(2):
            if done is None:
                packed = sum_s0[h].finish()
            else:
                packed = get(done.at[h], mc, hq)
            halves.append(unpack(packed, q).astype(BF))
        sol[which] = jnp.concatenate(halves, axis=1)
    upd[...] = (arhs[...].astype(F32) - sum_u.finish()).astype(BF)
    for cp in pending:
        cp.wait_send()


def on_device(diag, panel_rhs, below, row_ids, ancestor_rhs, ancestor_solution):
    n, m = lax.axis_size("row"), lax.axis_size("col")
    z = sizes_of(n, m, diag, panel_rhs, below, row_ids, ancestor_rhs)
    nz, b, q = z["nz"], z["b"], z["q"]
    cc, p, cap, bs, nrhs, na, pb = (z[k] for k in ("cc", "p", "cap", "bs", "nrhs", "na", "pb"))
    a, ab = z["a"], z["ab"]
    row = lax.axis_index("row")

    def slot_of(ids, wanted):
        found = ids[None, :] == wanted[:, None]
        return jnp.min(jnp.where(found, jnp.arange(cap)[None, :], cap), axis=1)

    def place_of(ids):
        position = ids - z["pw"] - row * na
        return jnp.where((position >= 0) & (position < na), position, na)

    later_ids = z["pw"] + row * na + jnp.arange(na)
    idx = jnp.concatenate([
        slot_of(row_ids[0], row * pb + jnp.arange(pb)),
        slot_of(row_ids[0], later_ids),
        slot_of(row_ids[1], later_ids),
        place_of(row_ids[0]),
        place_of(row_ids[1]),
    ]).astype(jnp.int32)

    vmem = pl.BlockSpec(memory_space=pltpu.VMEM)
    hbm = pl.BlockSpec(memory_space=pl.ANY)
    nsem = 14 * 2 * nz + 12 * m
    V = pltpu.VMEM
    return pl.pallas_call(
        functools.partial(kernel, z),
        out_shape=(
            jax.ShapeDtypeStruct((2, q, nrhs), BF),
            jax.ShapeDtypeStruct((a, nrhs), BF),
        ),
        in_specs=[pl.BlockSpec(memory_space=pltpu.SMEM), hbm, vmem, hbm, vmem, vmem],
        out_specs=(vmem, vmem),
        scratch_shapes=[
            V((cc, p), BF), V((cc, p), BF),
            V((cap + 1, bs, cc), BF), V((cap, bs, cc), BF), V((pb, bs, cc), BF),
            V((na + 1, bs, nrhs), BF), V((nrhs, max(cap, pb) * bs), BF),
            V((2, cap + 1, bs, nrhs), F32), V((nrhs, cc), F32),
            V((cc, nrhs), BF), V((cc, nrhs), BF), V((2, cc, nrhs), BF),
        ] + [V((2, cc // 2, nrhs), BF)] * 6 + [V((3, 2, nz, b // 2, nrhs), BF)] * 3 + [
            V((nz, b, nrhs), BF)
        ] * 3 + [V((2, p // 2, nrhs), BF)] * 5 + [
            V((na * bs, nrhs), BF),
            V((3, 2, m, q // 2, nrhs), BF), V((m, a, nrhs), BF),
            pltpu.SemaphoreType.DMA((4,)),
            pltpu.SemaphoreType.DMA((nsem,)),
            pltpu.SemaphoreType.DMA((nsem,)),
        ],
        compiler_params=pltpu.CompilerParams(
            collective_id=0, has_side_effects=True, vmem_limit_bytes=62 * 1024 * 1024
        ),
    )(
        idx, diag, panel_rhs, below.reshape(2, cap, bs, cc), ancestor_rhs,
        ancestor_solution.reshape(ab, bs, nrhs),
    )


def solution(mesh):
    in_specs = (
        P(None, "col", "row"),
        P(None, "row", None),
        P(None, "row", "col"),
        P(None, "row"),
        P(("row", "col"), None),
        P(("row", "col"), None),
    )
    out_specs = (P(None, ("row", "col"), None), P(("row", "col"), None))
    return jax.shard_map(
        on_device, mesh=mesh, in_specs=in_specs, out_specs=out_specs, check_vma=False
    )
```
